32 devices in a mesh: shard: 4 (over x, core), replica: 8 (over z, y).
Axes of the slice: x: 2, y: 2, z: 4, core: 2. Of those that a mesh axis runs over, the one named last changes fastest.
Arguments:
- gradients: bfloat16 [8, 32, 512, 512], P('replica', 'shard'), may hold values from -3 to 3
- first_moment: float32 [32, 512, 512], P(('shard', 'replica')), may hold values from -6 to 6
- second_moment: float32 [32, 512, 512], P(('shard', 'replica')), may hold values from 0.25 to 4
- left_stat: float32 [32, 512, 512], P(('shard', 'replica')), as said below
- right_stat: float32 [32, 512, 512], P(('shard', 'replica')), as said below
- left_basis: float32 [32, 512, 512], P(('shard', 'replica')), as said below
- right_basis: float32 [32, 512, 512], P(('shard', 'replica')), as said below
- refresh_flags: int32 [32], replicated, may hold values from 0 to 1, as said below
Outputs:
- direction: bfloat16 [32, 512, 512], P('shard')
- new_first: float32 [32, 512, 512], P(('shard', 'replica'))
- new_second: float32 [32, 512, 512], P(('shard', 'replica'))
- new_left: float32 [32, 512, 512], P(('shard', 'replica'))
- new_right: float32 [32, 512, 512], P(('shard', 'replica'))
- new_left_basis: float32 [32, 512, 512], P(('shard', 'replica'))
- new_right_basis: float32 [32, 512, 512], P(('shard', 'replica'))
The draws below stay inside these ranges and needn't reach their ends.
Inputs may be any that keep to these rules, and one draw needn't show every extreme that they name: Write b = ((p * 8 + q)) + j. For every q, j and k, exactly one of the two blocks with p = 2 k and p = 2 k + 1 has refresh_flags[b] = 1. `left_stat`: every block is symmetric positive definite with all eigenvalues 1 or more. `right_stat`: every block is symmetric positive definite with all eigenvalues 1 or more. `left_basis`: every block is an orthogonal matrix. `right_basis`: every block is an orthogonal matrix.
All inputs are finite; a program needn't handle non-finite values.
Results may differ from the reference program's by a relative error of at most 0.012.
Values may be sent and summed in bfloat16 or wider, within the bound.
A program may use at most 128 MiB of HBM per device.

```python
import math
import jax
import jax.numpy as jnp
from jax import lax

BLOCK = 512
BLK_DEV = 1
POWER = 2
NBLK = 32
N_SHARD = 4
N_REPLICA = 8


def definite_blocks(key):
    key_diag, key_factor = jax.random.split(key)
    diagonal = jnp.exp(jax.random.uniform(key_diag, (NBLK, BLOCK), jnp.float32, 0.0, jnp.log(10.0)))
    factor = jax.random.normal(key_factor, (NBLK, BLOCK, BLOCK), jnp.float32)
    square = jnp.einsum('kij,klj->kil', factor, factor, precision=lax.Precision.HIGHEST) * (0.5 / BLOCK)
    square = 0.5 * (square + jnp.swapaxes(square, 1, 2))
    return square + jnp.eye(BLOCK, dtype=jnp.float32)[None, :, :] * diagonal[:, :, None]


def orthogonal_blocks(key):
    matrix = jax.random.normal(key, (NBLK, BLOCK, BLOCK), jnp.float32)
    basis, upper = jnp.linalg.qr(matrix)
    return basis


def draw_left_stat(key, part):
    return definite_blocks(jax.random.fold_in(key, 101))


def draw_right_stat(key, part):
    return definite_blocks(jax.random.fold_in(key, 102))


def draw_left_basis(key, part):
    return orthogonal_blocks(jax.random.fold_in(key, 103))


def draw_right_basis(key, part):
    return orthogonal_blocks(jax.random.fold_in(key, 104))


def draw_refresh_flags(key, part):
    picks = jax.random.randint(jax.random.fold_in(key, 105), (N_SHARD // 2, N_REPLICA, BLK_DEV), 0, 2)
    shard_ids = jnp.arange(N_SHARD, dtype=jnp.int32)
    chosen = picks[shard_ids // 2]
    flagged = (chosen == (shard_ids % 2)[:, None, None]).astype(jnp.int32)
    return flagged.reshape(NBLK)


def block_scale(own_key, dims, cuts, least, high):
    level = 1.0
    for dim, blocks in cuts:
        draws = jax.random.uniform(jax.random.fold_in(jax.random.fold_in(own_key, 6), dim), (blocks,), jnp.float32, least / len(cuts), high / len(cuts))
        level = level * jnp.repeat(jnp.exp(draws), dims[dim] // blocks).reshape((-1,) + (1,) * (len(dims) - 1 - dim))
    return level


def scatter_about(stream_key, shape, width, limit, cuts=(), kind=jnp.bfloat16):
    values = width * jax.random.normal(stream_key, shape, jnp.float32)
    if cuts:
        values = values * block_scale(stream_key, shape, cuts, -0.22, 0.18)
    return jnp.clip(values, -limit, limit).astype(kind)


def setup_inputs(seed: int = 0) -> dict:
    seeds = jax.random.split(jax.random.key(seed), 9)
    gradients = scatter_about(seeds[0], (N_REPLICA, NBLK, BLOCK, BLOCK), 0.5, 3.0, ((0, 8), (1, 4)))
    first_moment = scatter_about(seeds[1], (NBLK, BLOCK, BLOCK), 1.0, 6.0, ((0, 32),), jnp.float32)
    second_moment = jnp.clip(jnp.exp(math.log(4.0) - 2.7725887 * jax.random.uniform(seeds[2], (NBLK, BLOCK, BLOCK), jnp.float32) ** block_scale(seeds[2], (NBLK, BLOCK, BLOCK), ((0, 32),), -0.2, 0.2)), 0.25, 4.0)
    left_stat = draw_left_stat(jax.random.fold_in(seeds[8], 71), 0)
    right_stat = draw_right_stat(jax.random.fold_in(seeds[8], 71), 0)
    left_basis = draw_left_basis(jax.random.fold_in(seeds[8], 71), 0)
    right_basis = draw_right_basis(jax.random.fold_in(seeds[8], 71), 0)
    refresh_flags = draw_refresh_flags(jax.random.fold_in(seeds[8], 71), 0)
    return dict(gradients=gradients, first_moment=first_moment, second_moment=second_moment, left_stat=left_stat, right_stat=right_stat, left_basis=left_basis, right_basis=right_basis, refresh_flags=refresh_flags)


beta_one = 0.95
beta_two = 0.95
epsilon = 1e-08
bias_step = 10.0

def highest(left_side, right_side):
    return jnp.dot(left_side.astype(jnp.float32), right_side.astype(jnp.float32), precision=lax.Precision.HIGHEST, preferred_element_type=jnp.float32)

def orthonormal(matrix):
    gram = highest(matrix.T, matrix)
    lower_factor = jnp.linalg.cholesky(gram)
    return jax.scipy.linalg.solve_triangular(lower_factor, matrix.T, lower=True).T

def power_step(factor, basis):
    for repeat in range(POWER):
        product = jnp.dot(factor.astype(jnp.bfloat16).astype(jnp.float32), basis.astype(jnp.bfloat16).astype(jnp.float32), preferred_element_type=jnp.float32)
        basis = orthonormal(product)
    return basis

def update_block(grad_stack, moment, second, left_factor, right_factor, basis_old_left, basis_old_right, flagged):
    summed = lax.optimization_barrier(jnp.sum(grad_stack.astype(jnp.float32), axis=0))
    low_grad = summed.astype(jnp.bfloat16)
    left_new = beta_two * left_factor + (1.0 - beta_two) / BLOCK * jnp.dot(low_grad.astype(jnp.float32), low_grad.T.astype(jnp.float32), preferred_element_type=jnp.float32)
    right_new = beta_two * right_factor + (1.0 - beta_two) / BLOCK * jnp.dot(low_grad.T.astype(jnp.float32), low_grad.astype(jnp.float32), preferred_element_type=jnp.float32)

    def refresh_both():
        basis_left = power_step(left_new, basis_old_left)
        basis_right = power_step(right_new, basis_old_right)
        carried = highest(highest(highest(basis_left.T, basis_old_left), moment), highest(basis_old_right.T, basis_right))
        return (basis_left, basis_right, carried)

    def retain():
        return (basis_old_left, basis_old_right, moment)
    basis_left, basis_right, carried = lax.cond(flagged == 1, refresh_both, retain)
    rotated = highest(highest(basis_left.T, summed), basis_right)
    moment_new = beta_one * carried + (1.0 - beta_one) * rotated
    second_new = beta_two * second + (1.0 - beta_two) * rotated * rotated
    scaled = moment_new / (1.0 - beta_one ** bias_step) / (jnp.sqrt(second_new / (1.0 - beta_two ** bias_step)) + epsilon)
    direction = highest(highest(basis_left, scaled), basis_right.T).astype(jnp.bfloat16)
    return (direction, moment_new, second_new, left_new, right_new, basis_left, basis_right)

def reference(gradients, first_moment, second_moment, left_stat, right_stat, left_basis, right_basis, refresh_flags):

    def handle(position):
        pieces = [lax.dynamic_index_in_dim(array, position, 0, keepdims=False) for array in (first_moment, second_moment, left_stat, right_stat, left_basis, right_basis)]
        grad_stack = lax.dynamic_index_in_dim(gradients, position, 1, keepdims=False)
        flagged = lax.dynamic_index_in_dim(refresh_flags, position, 0, keepdims=False)
        return update_block(grad_stack, pieces[0], pieces[1], pieces[2], pieces[3], pieces[4], pieces[5], flagged)
    results = lax.map(handle, jnp.arange(NBLK, dtype=jnp.int32))
    return (results[0], results[1], results[2], results[3], results[4], results[5], results[6])
```

```python
import functools

import jax
import jax.numpy as jnp
from jax import lax
from jax.experimental import pallas as pl
from jax.experimental.pallas import tpu as pltpu
from jax.sharding import PartitionSpec as P

POWER = 2


beta_one = 0.95
beta_two = 0.95
epsilon = 1e-08
bias_step = 10.0

TILE = 128
ROWS = 8


def paired(block):
    count = lax.axis_size("shard")
    return lax.ppermute(block, "shard", [(low, low ^ 1) for low in range(count)])


def product(left_side, right_side, contract=(1, 0), precision=lax.Precision.HIGHEST):
    return lax.dot_general(
        left_side,
        right_side,
        (((contract[0],), (contract[1],)), ((), ())),
        precision=precision,
        preferred_element_type=jnp.float32,
    )


def low_product(left_side, right_side, contract=(1, 0)):
    return product(
        left_side.astype(jnp.bfloat16), right_side.astype(jnp.bfloat16), contract, None
    )


def inverse_factor(tile):
    side = tile.shape[0]
    spread = (ROWS, side)
    lane = lax.broadcasted_iota(jnp.int32, spread, 1)
    sub = lax.broadcasted_iota(jnp.int32, spread, 0)
    count = side // ROWS
    groups = [tile[ROWS * g : ROWS * (g + 1), :] for g in range(count)]
    finished = []
    for step in range(count):
        start = ROWS * step
        head = groups[step]
        inside = (lane >= start) & (lane < start + ROWS)
        columns = [
            jnp.broadcast_to(head[:, start + j : start + j + 1], spread) for j in range(ROWS)
        ]
        small = [
            [jnp.broadcast_to(columns[j][i : i + 1, :], spread) for j in range(i + 1)]
            for i in range(ROWS)
        ]
        lines = [
            jnp.where(
                lane == start + i,
                1.0,
                jnp.where(inside, 0.0, jnp.broadcast_to(head[i : i + 1, :], spread)),
            )
            for i in range(ROWS)
        ]
        factor = [[None] * ROWS for _ in range(ROWS)]
        inverse = []
        for j in range(ROWS):
            inverse.append(1.0 / small[j][j])
            for i in range(j + 1, ROWS):
                factor[i][j] = small[i][j] * inverse[j]
            for i in range(j + 1, ROWS):
                lines[i] = lines[i] - factor[i][j] * lines[j]
                for t in range(j + 1, i + 1):
                    small[i][t] = small[i][t] - factor[i][j] * small[t][j]
        done = jnp.zeros(spread, jnp.float32)
        for j in range(ROWS):
            done = jnp.where(sub == j, lines[j] * lax.rsqrt(small[j][j]), done)
        finished.append(jnp.where(lane < start + ROWS, done, 0.0))
        if step + 1 == count:
            break
        back = [None] * ROWS
        for j in reversed(range(ROWS)):
            value = lines[j] * inverse[j]
            for i in reversed(range(j + 1, ROWS)):
                value = value - factor[i][j] * back[i]
            back[j] = value
        for g in range(step + 1, count):
            old = groups[g]
            terms = [
                jnp.broadcast_to(old[:, start + j : start + j + 1], spread) * back[j]
                for j in range(ROWS)
            ]
            while len(terms) > 1:
                terms = [terms[t] + terms[t + 1] for t in range(0, len(terms), 2)]
            groups[g] = jnp.where(inside, 0.0, old) - terms[0]
    return jnp.concatenate(finished, 0)


def refresh_kernel(factor_ref, turned_ref, out_ref, joint):
    side = factor_ref.shape[0]
    out_ref[...] = turned_ref[...].astype(jnp.float32)

    def repeat(_, carry):
        turned = product(out_ref[...].astype(jnp.bfloat16), factor_ref[...], precision=None)
        joint[:, side:] = turned
        joint[:, :side] = product(turned, turned, (1, 1))

        for block in range(side // TILE):
            at = block * TILE
            rows = pl.ds(at, TILE)
            inverse = inverse_factor(joint[rows, pl.ds(at, TILE)])
            fresh = product(inverse, joint[rows, side:])
            out_ref[rows, :] = fresh
            if at + TILE < side:
                rest = pl.ds(at + TILE, side - at - TILE)
                below = product(joint[rest, pl.ds(at, TILE)], inverse, (1, 1))
                joint[rest, rest] -= product(below, below, (1, 1))
                joint[rest, side:] -= product(below, fresh)
        return carry

    lax.fori_loop(0, POWER, repeat, 0)


def refresh(factor, turned):
    side = factor.shape[0]
    return pl.pallas_call(
        refresh_kernel,
        out_shape=jax.ShapeDtypeStruct((side, side), jnp.float32),
        in_specs=[pl.BlockSpec(memory_space=pltpu.VMEM)] * 2,
        out_specs=pl.BlockSpec(memory_space=pltpu.VMEM),
        scratch_shapes=[pltpu.VMEM((side, 2 * side), jnp.float32)],
        name="refresh",
    )(factor, turned)


def local(
    gradients,
    first_moment,
    second_moment,
    left_stat,
    right_stat,
    left_basis,
    right_basis,
    refresh_flags,
):
    replica_count = lax.axis_size("replica")
    owner_id = lax.axis_index("shard") * replica_count + lax.axis_index("replica")
    listed = lax.dynamic_index_in_dim(refresh_flags, owner_id, 0, keepdims=False) == 1
    moment, second = first_moment[0], second_moment[0]
    basis_left, basis_right = left_basis[0], right_basis[0]
    plain = low_product(low_product(basis_left, moment), basis_right, (1, 1))
    summed = lax.psum_scatter(gradients, "replica", scatter_dimension=1, tiled=True)[0, 0]
    low_grad = summed.astype(jnp.bfloat16)
    block_side = low_grad.shape[0]
    rate = (1.0 - beta_two) / block_side
    right_new = beta_two * right_stat[0] + rate * low_product(low_grad, low_grad, (0, 0))
    left_new = beta_two * left_stat[0] + rate * low_product(low_grad, low_grad, (1, 1))
    incoming = paired(jnp.stack([right_new, basis_right.T], 0).astype(jnp.bfloat16))
    chosen = jnp.where(
        listed, jnp.stack([left_new, basis_left.T], 0).astype(jnp.bfloat16), incoming
    )
    turned = refresh(chosen[0], chosen[1])
    arrived = paired(turned.astype(jnp.bfloat16))
    new_left = jnp.where(listed, turned.T, basis_left)
    new_right = jnp.where(listed, arrived.T.astype(jnp.float32), basis_right)
    both = jnp.concatenate([plain.astype(jnp.bfloat16), low_grad], 1)
    half = low_product(new_left, both, (0, 0))
    carried = jnp.where(listed, low_product(half[:, :block_side], new_right), moment)
    rotated = low_product(half[:, block_side:], new_right)
    moment_new = beta_one * carried + (1.0 - beta_one) * rotated
    second_new = beta_two * second + (1.0 - beta_two) * rotated * rotated
    scaled = (
        moment_new
        / (1.0 - beta_one**bias_step)
        / (jnp.sqrt(second_new / (1.0 - beta_two**bias_step)) + epsilon)
    )
    outward = low_product(low_product(new_left, scaled), new_right, (1, 1))
    gathered = lax.all_gather(outward.astype(jnp.bfloat16)[None], "replica", axis=0, tiled=True)
    return (
        gathered,
        moment_new[None],
        second_new[None],
        left_new[None],
        right_new[None],
        new_left[None],
        new_right[None],
    )


def solution(mesh):
    owned = P(("shard", "replica"), None, None)
    in_specs = (P("replica", "shard", None, None),) + (owned,) * 6 + (P(),)
    out_specs = (P("shard", None, None),) + (owned,) * 6
    return jax.shard_map(local, mesh=mesh, in_specs=in_specs, out_specs=out_specs, check_vma=False)
```

```python
import jax
import jax.numpy as jnp
from jax import lax
from jax.experimental import pallas as pl
from jax.experimental.pallas import tpu as pltpu
from jax.sharding import PartitionSpec as P

POWER = 2


beta_one = 0.95
beta_two = 0.95
epsilon = 1e-08
bias_step = 10.0

TILE = 128
ROWS = 8
CHUNKS = 2
MESH = pl.DeviceIdType.MESH


def paired(block):
    count = lax.axis_size("shard")
    return lax.ppermute(block, "shard", [(low, low ^ 1) for low in range(count)])


def product(left_side, right_side, contract=(1, 0), precision=lax.Precision.HIGHEST):
    return lax.dot_general(
        left_side,
        right_side,
        (((contract[0],), (contract[1],)), ((), ())),
        precision=precision,
        preferred_element_type=jnp.float32,
    )


def low_product(left_side, right_side, contract=(1, 0)):
    return product(
        left_side.astype(jnp.bfloat16), right_side.astype(jnp.bfloat16), contract, None
    )


def inverse_factor(tile):
    side = tile.shape[0]
    spread = (ROWS, side)
    lane = lax.broadcasted_iota(jnp.int32, spread, 1)
    sub = lax.broadcasted_iota(jnp.int32, spread, 0)
    count = side // ROWS
    groups = [tile[ROWS * g : ROWS * (g + 1), :] for g in range(count)]
    finished = []
    for step in range(count):
        start = ROWS * step
        head = groups[step]
        inside = (lane >= start) & (lane < start + ROWS)
        columns = [
            jnp.broadcast_to(head[:, start + j : start + j + 1], spread) for j in range(ROWS)
        ]
        small = [
            [jnp.broadcast_to(columns[j][i : i + 1, :], spread) for j in range(i + 1)]
            for i in range(ROWS)
        ]
        lines = [
            jnp.where(
                lane == start + i,
                1.0,
                jnp.where(inside, 0.0, jnp.broadcast_to(head[i : i + 1, :], spread)),
            )
            for i in range(ROWS)
        ]
        factor = [[None] * ROWS for _ in range(ROWS)]
        inverse = []
        for j in range(ROWS):
            inverse.append(1.0 / small[j][j])
            for i in range(j + 1, ROWS):
                factor[i][j] = small[i][j] * inverse[j]
            for i in range(j + 1, ROWS):
                lines[i] = lines[i] - factor[i][j] * lines[j]
                for t in range(j + 1, i + 1):
                    small[i][t] = small[i][t] - factor[i][j] * small[t][j]
        done = jnp.zeros(spread, jnp.float32)
        for j in range(ROWS):
            done = jnp.where(sub == j, lines[j] * lax.rsqrt(small[j][j]), done)
        finished.append(jnp.where(lane < start + ROWS, done, 0.0))
        if step + 1 == count:
            break
        back = [None] * ROWS
        for j in reversed(range(ROWS)):
            value = lines[j] * inverse[j]
            for i in reversed(range(j + 1, ROWS)):
                value = value - factor[i][j] * back[i]
            back[j] = value
        for g in range(step + 1, count):
            old = groups[g]
            terms = [
                jnp.broadcast_to(old[:, start + j : start + j + 1], spread) * back[j]
                for j in range(ROWS)
            ]
            while len(terms) > 1:
                terms = [terms[t] + terms[t + 1] for t in range(0, len(terms), 2)]
            groups[g] = jnp.where(inside, 0.0, old) - terms[0]
    return jnp.concatenate(finished, 0)


def refresh_kernel(listed_ref, left_ref, left_basis_ref, incoming_ref, turned_ref, basis_ref, held, joint):
    side = left_ref.shape[0]
    listed = listed_ref[0] == 1

    @pl.when(listed)
    def _():
        held[...] = left_basis_ref[...].T

    @pl.when(jnp.logical_not(listed))
    def _():
        held[...] = incoming_ref[1].astype(jnp.float32).T

    factor = jnp.where(
        jnp.full((side, side), listed_ref[0], jnp.int32) == 1,
        left_ref[...].astype(jnp.float32),
        incoming_ref[0].astype(jnp.float32),
    ).astype(jnp.bfloat16)
    turned_ref[...] = factor

    def repeat(_, carry):
        turned = product(held[...].astype(jnp.bfloat16), turned_ref[...], precision=None)
        joint[:, side:] = turned
        joint[:, :side] = product(turned, turned, (1, 1))

        for block in range(side // TILE):
            at = block * TILE
            rows = pl.ds(at, TILE)
            inverse = inverse_factor(joint[rows, pl.ds(at, TILE)])
            fresh = product(inverse, joint[rows, side:])
            held[rows, :] = fresh
            if at + TILE < side:
                rest = pl.ds(at + TILE, side - at - TILE)
                below = product(joint[rest, pl.ds(at, TILE)], inverse, (1, 1))
                joint[rest, rest] -= product(below, below, (1, 1))
                joint[rest, side:] -= product(below, fresh)
        return carry

    lax.fori_loop(0, POWER, repeat, 0)
    turned_ref[...] = held[...].T.astype(jnp.bfloat16)

    @pl.when(listed)
    def _():
        basis_ref[...] = held[...].T

    @pl.when(jnp.logical_not(listed))
    def _():
        basis_ref[...] = left_basis_ref[...]


def statistics_kernel(grad_ref, left_ref, right_ref, basis_ref, left_out, right_out, low_out, send_out):
    grad = grad_ref[...]
    rate = (1.0 - beta_two) / grad.shape[0]
    left = beta_two * left_ref[...] + rate * low_product(grad, grad, (1, 1))
    left_out[...] = left
    low_out[...] = left.astype(jnp.bfloat16)
    right = beta_two * right_ref[...] + rate * low_product(grad, grad, (0, 0))
    right_out[...] = right
    send_out[0] = right.astype(jnp.bfloat16)
    send_out[1] = basis_ref[...].astype(jnp.bfloat16)


def update_kernel(
    listed_ref,
    grad_ref,
    moment_ref,
    second_ref,
    old_left_ref,
    old_right_ref,
    left_ref,
    arrived_ref,
    moment_out,
    second_out,
    right_out,
    direction_out,
):
    listed = listed_ref[0] == 1

    @pl.when(listed)
    def _():
        right_out[...] = arrived_ref[...].astype(jnp.float32)
        plain = low_product(
            low_product(old_left_ref[...], moment_ref[...]), old_right_ref[...], (1, 1)
        )
        moment_out[...] = low_product(
            low_product(left_ref[...], plain, (0, 0)), arrived_ref[...]
        )

    @pl.when(jnp.logical_not(listed))
    def _():
        right_out[...] = old_right_ref[...]
        moment_out[...] = moment_ref[...]

    left = left_ref[...].astype(jnp.bfloat16)
    right = right_out[...].astype(jnp.bfloat16)
    rotated = low_product(low_product(left, grad_ref[...], (0, 0)), right)
    moment_new = beta_one * moment_out[...] + (1.0 - beta_one) * rotated
    second_new = beta_two * second_ref[...] + (1.0 - beta_two) * rotated * rotated
    moment_out[...] = moment_new
    second_out[...] = second_new
    scaled = (
        moment_new
        / (1.0 - beta_one**bias_step)
        / (jnp.sqrt(second_new / (1.0 - beta_two**bias_step)) + epsilon)
    )
    direction_out[...] = low_product(low_product(left, scaled), right, (1, 1)).astype(
        jnp.bfloat16
    )


def sequence(outer_count):
    return sorted(range(outer_count), key=lambda m: (m == 0, abs(2 * m - outer_count), m))


def place(outer_count):
    me = lax.axis_index("replica")
    inner = lax.rem(me, 2)
    return me, inner, me // 2, me + 1 - 2 * inner


def meet(outer_count):
    me, inner, outer, partner = place(outer_count)
    barrier = pltpu.get_barrier_semaphore()
    pl.semaphore_signal(barrier, inc=1, device_id={"replica": partner}, device_id_type=MESH)
    for m in range(1, outer_count):
        other = lax.rem(outer + m, outer_count) * 2 + inner
        pl.semaphore_signal(barrier, inc=1, device_id={"replica": other}, device_id_type=MESH)
    pl.semaphore_wait(barrier, outer_count)


def remote(source, target, send_sem, recv_sem, replica):
    return pltpu.make_async_remote_copy(
        src_ref=source,
        dst_ref=target,
        send_sem=send_sem,
        recv_sem=recv_sem,
        device_id={"replica": replica},
        device_id_type=MESH,
    )


def sum_kernel(
    grad_ref, out_ref, mine, got, pairs, far, load_sem, near_send, near_recv, far_send, far_recv
):
    outer_count = mine.shape[0]
    rows = mine.shape[1] // CHUNKS
    me, inner, outer, partner = place(outer_count)
    meet(outer_count)
    order = sequence(outer_count)
    near, loads = {}, {}
    for m in order:
        aim = lax.rem(outer + m, outer_count)
        for c in range(CHUNKS):
            part = pl.ds(c * rows, rows)
            near[m, c] = remote(
                grad_ref.at[0, aim * 2 + 1 - inner, part],
                got.at[m, part],
                near_send.at[m, c],
                near_recv.at[m, c],
                partner,
            )
            near[m, c].start()
        loads[m] = pltpu.make_async_copy(
            grad_ref.at[0, aim * 2 + inner], mine.at[m], load_sem.at[m]
        )
        loads[m].start()
    away = {}
    for m in order:
        aim = lax.rem(outer + m, outer_count)
        loads[m].wait()
        for c in range(CHUNKS):
            part = pl.ds(c * rows, rows)
            near[m, c].wait_recv()
            total = mine[m, part].astype(jnp.float32) + got[m, part].astype(jnp.float32)
            if m != 0:
                pairs[m, part] = total.astype(jnp.bfloat16)
                away[m, c] = remote(
                    pairs.at[m, part],
                    far.at[m, part],
                    far_send.at[m, c],
                    far_recv.at[m, c],
                    aim * 2 + inner,
                )
                away[m, c].start()
    for c in range(CHUNKS):
        part = pl.ds(c * rows, rows)
        total = mine[0, part].astype(jnp.float32) + got[0, part].astype(jnp.float32)
        for m in order[:-1]:
            away[m, c].wait_recv()
            total = total + far[m, part].astype(jnp.float32)
        out_ref[part] = total.astype(jnp.bfloat16)
    for copy in list(near.values()) + list(away.values()):
        copy.wait_send()


def gather_kernel(block_ref, out_ref, own_sem, near_send, near_recv, far_send, far_recv):
    outer_count = out_ref.shape[0] // 2
    rows = block_ref.shape[0] // CHUNKS
    me, inner, outer, partner = place(outer_count)
    meet(outer_count)
    order = sequence(outer_count)
    keep = pltpu.make_async_copy(block_ref, out_ref.at[me], own_sem.at[0])
    keep.start()
    near, away = {}, {}
    for m in order:
        aim = lax.rem(outer + m, outer_count)
        for c in range(CHUNKS):
            part = pl.ds(c * rows, rows)
            sems = (near_send, near_recv) if m == 0 else (far_send, far_recv)
            copy = remote(
                block_ref.at[part],
                out_ref.at[me, part],
                sems[0].at[m, c],
                sems[1].at[m, c],
                partner if m == 0 else aim * 2 + inner,
            )
            copy.start()
            (near if m == 0 else away)[m, c] = copy
    for c in range(CHUNKS):
        for m in order[:-1]:
            part = pl.ds(c * rows, rows)
            source = lax.rem(outer + outer_count - m, outer_count) * 2 + inner
            away[m, c].wait_recv()
            near[m, c] = remote(
                out_ref.at[source, part],
                out_ref.at[source, part],
                near_send.at[m, c],
                near_recv.at[m, c],
                partner,
            )
            near[m, c].start()
    for copy in near.values():
        copy.wait_recv()
    for copy in list(near.values()) + list(away.values()):
        copy.wait_send()
    keep.wait()


VMEM = pl.BlockSpec(memory_space=pltpu.VMEM)
SMEM = pl.BlockSpec(memory_space=pltpu.SMEM)
ANY = pl.BlockSpec(memory_space=pl.ANY)


def replica_sum(gradients):
    count, side = gradients.shape[1], gradients.shape[2]
    outer = count // 2
    held = pltpu.VMEM((outer, side, side), jnp.bfloat16)
    flags = pltpu.SemaphoreType.DMA((outer, CHUNKS))
    return pl.pallas_call(
        sum_kernel,
        out_shape=jax.ShapeDtypeStruct((side, side), jnp.bfloat16),
        in_specs=[ANY],
        out_specs=VMEM,
        scratch_shapes=[held] * 4 + [pltpu.SemaphoreType.DMA((outer,))] + [flags] * 4,
        compiler_params=pltpu.CompilerParams(collective_id=0, has_side_effects=True),
        name="replica_sum",
    )(gradients)


def replica_gather(block, count):
    side = block.shape[0]
    flags = pltpu.SemaphoreType.DMA((count // 2, CHUNKS))
    return pl.pallas_call(
        gather_kernel,
        out_shape=jax.ShapeDtypeStruct((count, side, side), jnp.bfloat16),
        in_specs=[VMEM],
        out_specs=ANY,
        scratch_shapes=[pltpu.SemaphoreType.DMA((1,))] + [flags] * 4,
        compiler_params=pltpu.CompilerParams(collective_id=1, has_side_effects=True),
        name="replica_gather",
    )(block)


def local(
    gradients,
    first_moment,
    second_moment,
    left_stat,
    right_stat,
    left_basis,
    right_basis,
    refresh_flags,
):
    replica_count = lax.axis_size("replica")
    owner_id = lax.axis_index("shard") * replica_count + lax.axis_index("replica")
    listed = lax.dynamic_slice_in_dim(refresh_flags, owner_id, 1)
    side = left_stat.shape[1]
    wide = jax.ShapeDtypeStruct((side, side), jnp.float32)
    low = jax.ShapeDtypeStruct((side, side), jnp.bfloat16)
    low_grad = replica_sum(gradients)
    left_new, right_new, left_low, outgoing = pl.pallas_call(
        statistics_kernel,
        out_shape=(wide, wide, low, jax.ShapeDtypeStruct((2, side, side), jnp.bfloat16)),
        in_specs=[VMEM] * 4,
        out_specs=(VMEM,) * 4,
        name="statistics",
    )(low_grad, left_stat[0], right_stat[0], right_basis[0])
    incoming = paired(outgoing)
    turned, new_left = pl.pallas_call(
        refresh_kernel,
        out_shape=(low, wide),
        in_specs=[SMEM] + [VMEM] * 3,
        out_specs=(VMEM,) * 2,
        scratch_shapes=[
            pltpu.VMEM((side, side), jnp.float32),
            pltpu.VMEM((side, 2 * side), jnp.float32),
        ],
        name="refresh",
    )(listed, left_low, left_basis[0], incoming)
    arrived = paired(turned)
    moment_new, second_new, new_right, outward = pl.pallas_call(
        update_kernel,
        out_shape=(wide, wide, wide, low),
        in_specs=[SMEM] + [VMEM] * 7,
        out_specs=(VMEM,) * 4,
        name="update",
    )(
        listed,
        low_grad,
        first_moment[0],
        second_moment[0],
        left_basis[0],
        right_basis[0],
        new_left,
        arrived,
    )
    gathered = replica_gather(outward, replica_count)
    return (
        gathered,
        moment_new[None],
        second_new[None],
        left_new[None],
        right_new[None],
        new_left[None],
        new_right[None],
    )


def solution(mesh):
    owned = P(("shard", "replica"), None, None)
    in_specs = (P("replica", "shard", None, None),) + (owned,) * 6 + (P(),)
    out_specs = (P("shard", None, None),) + (owned,) * 6
    return jax.shard_map(local, mesh=mesh, in_specs=in_specs, out_specs=out_specs, check_vma=False)
```

```python
import jax
import jax.numpy as jnp
from jax import lax
from jax.experimental import pallas as pl
from jax.experimental.pallas import tpu as pltpu
from jax.sharding import PartitionSpec as P

POWER = 2


beta_one = 0.95
beta_two = 0.95
epsilon = 1e-08
bias_step = 10.0

TILE = 128
ROWS = 8
CHUNKS = 4
MESH = pl.DeviceIdType.MESH


def paired(block):
    count = lax.axis_size("shard")
    return lax.ppermute(block, "shard", [(low, low ^ 1) for low in range(count)])


def product(left_side, right_side, contract=(1, 0), precision=lax.Precision.HIGHEST):
    return lax.dot_general(
        left_side,
        right_side,
        (((contract[0],), (contract[1],)), ((), ())),
        precision=precision,
        preferred_element_type=jnp.float32,
    )


def low_product(left_side, right_side, contract=(1, 0)):
    return product(
        left_side.astype(jnp.bfloat16), right_side.astype(jnp.bfloat16), contract, None
    )


def inverse_factor(tile):
    side = tile.shape[0]
    spread = (ROWS, side)
    lane = lax.broadcasted_iota(jnp.int32, spread, 1)
    sub = lax.broadcasted_iota(jnp.int32, spread, 0)
    count = side // ROWS
    groups = [tile[ROWS * g : ROWS * (g + 1), :] for g in range(count)]
    finished = []
    for step in range(count):
        start = ROWS * step
        head = groups[step]
        inside = (lane >= start) & (lane < start + ROWS)
        columns = [
            jnp.broadcast_to(head[:, start + j : start + j + 1], spread) for j in range(ROWS)
        ]
        small = [
            [jnp.broadcast_to(columns[j][i : i + 1, :], spread) for j in range(i + 1)]
            for i in range(ROWS)
        ]
        lines = [
            jnp.where(
                lane == start + i,
                1.0,
                jnp.where(inside, 0.0, jnp.broadcast_to(head[i : i + 1, :], spread)),
            )
            for i in range(ROWS)
        ]
        factor = [[None] * ROWS for _ in range(ROWS)]
        inverse = []
        for j in range(ROWS):
            inverse.append(1.0 / small[j][j])
            for i in range(j + 1, ROWS):
                factor[i][j] = small[i][j] * inverse[j]
            for i in range(j + 1, ROWS):
                lines[i] = lines[i] - factor[i][j] * lines[j]
                for t in range(j + 1, i + 1):
                    small[i][t] = small[i][t] - factor[i][j] * small[t][j]
        done = jnp.zeros(spread, jnp.float32)
        for j in range(ROWS):
            done = jnp.where(sub == j, lines[j] * lax.rsqrt(small[j][j]), done)
        finished.append(jnp.where(lane < start + ROWS, done, 0.0))
        if step + 1 == count:
            break
        back = [None] * ROWS
        for j in reversed(range(ROWS)):
            value = lines[j] * inverse[j]
            for i in reversed(range(j + 1, ROWS)):
                value = value - factor[i][j] * back[i]
            back[j] = value
        for g in range(step + 1, count):
            old = groups[g]
            terms = [
                jnp.broadcast_to(old[:, start + j : start + j + 1], spread) * back[j]
                for j in range(ROWS)
            ]
            while len(terms) > 1:
                terms = [terms[t] + terms[t + 1] for t in range(0, len(terms), 2)]
            groups[g] = jnp.where(inside, 0.0, old) - terms[0]
    return jnp.concatenate(finished, 0)


def refresh_kernel(listed_ref, left_ref, left_basis_ref, incoming_ref, turned_ref, basis_ref, held, joint):
    side = left_ref.shape[0]
    listed = listed_ref[0] == 1

    @pl.when(listed)
    def _():
        held[...] = left_basis_ref[...].T

    @pl.when(jnp.logical_not(listed))
    def _():
        held[...] = incoming_ref[1].astype(jnp.float32).T

    factor = jnp.where(
        jnp.full((side, side), listed_ref[0], jnp.int32) == 1,
        left_ref[...].astype(jnp.float32),
        incoming_ref[0].astype(jnp.float32),
    ).astype(jnp.bfloat16)
    turned_ref[...] = factor

    def repeat(_, carry):
        turned = product(held[...].astype(jnp.bfloat16), turned_ref[...], precision=None)
        joint[:, side:] = turned
        joint[:, :side] = product(turned, turned, (1, 1))

        tile = joint[:TILE, :TILE]
        for block in range(side // TILE):
            at, after = block * TILE, (block + 1) * TILE
            inverse = inverse_factor(tile)
            if after < side:
                near = product(joint[after : after + TILE, at:after], inverse, (1, 1))
                tile = joint[after : after + TILE, after : after + TILE] - product(
                    near, near, (1, 1)
                )
            fresh = product(inverse, joint[at:after, side:])
            held[at:after, :] = fresh
            if after < side:
                joint[after : after + TILE, side:] -= product(near, fresh)
            if after + TILE < side:
                below = product(joint[after + TILE :, at:after], inverse, (1, 1))
                joint[after + TILE :, after : after + TILE] -= product(below, near, (1, 1))
                joint[after + TILE :, after + TILE : side] -= product(below, below, (1, 1))
                joint[after + TILE :, side:] -= product(below, fresh)
        return carry

    lax.fori_loop(0, POWER, repeat, 0)
    turned_ref[...] = held[...].T.astype(jnp.bfloat16)

    @pl.when(listed)
    def _():
        basis_ref[...] = held[...].T

    @pl.when(jnp.logical_not(listed))
    def _():
        basis_ref[...] = left_basis_ref[...]


def statistics_kernel(grad_ref, left_ref, right_ref, basis_ref, left_out, right_out, low_out, send_out):
    grad = grad_ref[...]
    rate = (1.0 - beta_two) / grad.shape[0]
    left = beta_two * left_ref[...] + rate * low_product(grad, grad, (1, 1))
    left_out[...] = left
    low_out[...] = left.astype(jnp.bfloat16)
    right = beta_two * right_ref[...] + rate * low_product(grad, grad, (0, 0))
    right_out[...] = right
    send_out[0] = right.astype(jnp.bfloat16)
    send_out[1] = basis_ref[...].astype(jnp.bfloat16)


def update_kernel(
    listed_ref,
    grad_ref,
    moment_ref,
    second_ref,
    old_left_ref,
    old_right_ref,
    left_ref,
    arrived_ref,
    moment_out,
    second_out,
    right_out,
    direction_out,
):
    listed = listed_ref[0] == 1

    @pl.when(listed)
    def _():
        right_out[...] = arrived_ref[...].astype(jnp.float32)
        plain = low_product(
            low_product(old_left_ref[...], moment_ref[...]), old_right_ref[...], (1, 1)
        )
        moment_out[...] = low_product(
            low_product(left_ref[...], plain, (0, 0)), arrived_ref[...]
        )

    @pl.when(jnp.logical_not(listed))
    def _():
        right_out[...] = old_right_ref[...]
        moment_out[...] = moment_ref[...]

    left = left_ref[...].astype(jnp.bfloat16)
    right = right_out[...].astype(jnp.bfloat16)
    rotated = low_product(low_product(left, grad_ref[...], (0, 0)), right)
    moment_new = beta_one * moment_out[...] + (1.0 - beta_one) * rotated
    second_new = beta_two * second_ref[...] + (1.0 - beta_two) * rotated * rotated
    moment_out[...] = moment_new
    second_out[...] = second_new
    scaled = (
        moment_new
        / (1.0 - beta_one**bias_step)
        / (jnp.sqrt(second_new / (1.0 - beta_two**bias_step)) + epsilon)
    )
    direction_out[...] = low_product(low_product(left, scaled), right, (1, 1)).astype(
        jnp.bfloat16
    )


def sequence(outer_count):
    return sorted(range(outer_count), key=lambda m: (m == 0, abs(2 * m - outer_count), m))


def place(outer_count):
    me = lax.axis_index("replica")
    inner = lax.rem(me, 2)
    return me, inner, me // 2, me + 1 - 2 * inner


def meet(outer_count):
    me, inner, outer, partner = place(outer_count)
    barrier = pltpu.get_barrier_semaphore()
    pl.semaphore_signal(barrier, inc=1, device_id={"replica": partner}, device_id_type=MESH)
    for m in range(1, outer_count):
        other = lax.rem(outer + m, outer_count) * 2 + inner
        pl.semaphore_signal(barrier, inc=1, device_id={"replica": other}, device_id_type=MESH)
    pl.semaphore_wait(barrier, outer_count)


def remote(source, target, send_sem, recv_sem, replica):
    return pltpu.make_async_remote_copy(
        src_ref=source,
        dst_ref=target,
        send_sem=send_sem,
        recv_sem=recv_sem,
        device_id={"replica": replica},
        device_id_type=MESH,
    )


def sum_kernel(
    grad_ref, out_ref, mine, got, pairs, far, load_sem, near_send, near_recv, far_send, far_recv
):
    outer_count = mine.shape[0]
    rows = mine.shape[1] // CHUNKS
    me, inner, outer, partner = place(outer_count)
    meet(outer_count)
    order = sequence(outer_count)
    near, loads = {}, {}
    for m in order:
        aim = lax.rem(outer + m, outer_count)
        for c in range(CHUNKS):
            part = pl.ds(c * rows, rows)
            near[m, c] = remote(
                grad_ref.at[0, aim * 2 + 1 - inner, part],
                got.at[m, part],
                near_send.at[m, c],
                near_recv.at[m, c],
                partner,
            )
            near[m, c].start()
        loads[m] = pltpu.make_async_copy(
            grad_ref.at[0, aim * 2 + inner], mine.at[m], load_sem.at[m]
        )
        loads[m].start()
    away = {}
    for m in order:
        aim = lax.rem(outer + m, outer_count)
        loads[m].wait()
        for c in range(CHUNKS):
            part = pl.ds(c * rows, rows)
            near[m, c].wait_recv()
            total = mine[m, part].astype(jnp.float32) + got[m, part].astype(jnp.float32)
            if m != 0:
                pairs[m, part] = total.astype(jnp.bfloat16)
                away[m, c] = remote(
                    pairs.at[m, part],
                    far.at[m, part],
                    far_send.at[m, c],
                    far_recv.at[m, c],
                    aim * 2 + inner,
                )
                away[m, c].start()
    for c in range(CHUNKS):
        part = pl.ds(c * rows, rows)
        total = mine[0, part].astype(jnp.float32) + got[0, part].astype(jnp.float32)
        for m in order[:-1]:
            away[m, c].wait_recv()
            total = total + far[m, part].astype(jnp.float32)
        out_ref[part] = total.astype(jnp.bfloat16)
    for copy in list(near.values()) + list(away.values()):
        copy.wait_send()


def gather_kernel(
    block_ref, out_ref, own_sem, near_send, near_recv, up_send, up_recv, down_send, down_recv
):
    outer_count = out_ref.shape[0] // 2
    rows = block_ref.shape[0] // CHUNKS
    me, inner, outer, partner = place(outer_count)
    meet(outer_count)
    keep = pltpu.make_async_copy(block_ref, out_ref.at[me], own_sem.at[0])
    keep.start()

    def above():
        return outer + 1 < outer_count

    def below():
        return outer >= 1

    def move(kind, distance, c):
        part = pl.ds(c * rows, rows)
        if kind == "up":
            sems, target, origin = (up_send, up_recv), me + 2, me - 2 * distance
        elif kind == "down":
            sems, target, origin = (down_send, down_recv), me - 2, me + 2 * distance
        else:
            sems, target, origin = (near_send, near_recv), partner, me + 2 * distance
        slot = distance + outer_count - 1 if kind == "near" else distance
        source = block_ref.at[part] if distance == 0 else out_ref.at[origin, part]
        return remote(
            source, out_ref.at[origin, part], sems[0].at[slot, c], sems[1].at[slot, c], target
        )

    for c in range(CHUNKS):
        pl.when(above())(move("up", 0, c).start)
        pl.when(below())(move("down", 0, c).start)
    for c in range(CHUNKS):
        move("near", 0, c).start()
    for distance in range(1, outer_count):
        for c in range(CHUNKS):

            @pl.when(outer >= distance)
            def _():
                move("up", distance - 1, c).wait_recv()
                pl.when(above())(move("up", distance, c).start)
                move("near", -distance, c).start()

            @pl.when(outer + distance < outer_count)
            def _():
                move("down", distance - 1, c).wait_recv()
                pl.when(below())(move("down", distance, c).start)
                move("near", distance, c).start()

    for distance in range(outer_count):
        for c in range(CHUNKS):

            @pl.when(outer >= distance)
            def _():
                move("near", -distance, c).wait()
                pl.when(above())(move("up", distance, c).wait_send)

            @pl.when(outer + distance < outer_count)
            def _():
                if distance:
                    move("near", distance, c).wait()
                pl.when(below())(move("down", distance, c).wait_send)

    keep.wait()


VMEM = pl.BlockSpec(memory_space=pltpu.VMEM)
SMEM = pl.BlockSpec(memory_space=pltpu.SMEM)
ANY = pl.BlockSpec(memory_space=pl.ANY)


def replica_sum(gradients):
    count, side = gradients.shape[1], gradients.shape[2]
    outer = count // 2
    held = pltpu.VMEM((outer, side, side), jnp.bfloat16)
    flags = pltpu.SemaphoreType.DMA((outer, CHUNKS))
    return pl.pallas_call(
        sum_kernel,
        out_shape=jax.ShapeDtypeStruct((side, side), jnp.bfloat16),
        in_specs=[ANY],
        out_specs=VMEM,
        scratch_shapes=[held] * 4 + [pltpu.SemaphoreType.DMA((outer,))] + [flags] * 4,
        compiler_params=pltpu.CompilerParams(collective_id=0, has_side_effects=True),
        name="replica_sum",
    )(gradients)


def replica_gather(block, count):
    side = block.shape[0]
    outer = count // 2
    flags = pltpu.SemaphoreType.DMA((outer, CHUNKS))
    wide = pltpu.SemaphoreType.DMA((2 * outer - 1, CHUNKS))
    return pl.pallas_call(
        gather_kernel,
        out_shape=jax.ShapeDtypeStruct((count, side, side), jnp.bfloat16),
        in_specs=[VMEM],
        out_specs=ANY,
        scratch_shapes=[pltpu.SemaphoreType.DMA((1,))] + [wide] * 2 + [flags] * 4,
        compiler_params=pltpu.CompilerParams(collective_id=1, has_side_effects=True),
        name="replica_gather",
    )(block)


def local(
    gradients,
    first_moment,
    second_moment,
    left_stat,
    right_stat,
    left_basis,
    right_basis,
    refresh_flags,
):
    replica_count = lax.axis_size("replica")
    owner_id = lax.axis_index("shard") * replica_count + lax.axis_index("replica")
    listed = lax.dynamic_slice_in_dim(refresh_flags, owner_id, 1)
    side = left_stat.shape[1]
    wide = jax.ShapeDtypeStruct((side, side), jnp.float32)
    low = jax.ShapeDtypeStruct((side, side), jnp.bfloat16)
    low_grad = replica_sum(gradients)
    left_new, right_new, left_low, outgoing = pl.pallas_call(
        statistics_kernel,
        out_shape=(wide, wide, low, jax.ShapeDtypeStruct((2, side, side), jnp.bfloat16)),
        in_specs=[VMEM] * 4,
        out_specs=(VMEM,) * 4,
        name="statistics",
    )(low_grad, left_stat[0], right_stat[0], right_basis[0])
    incoming = paired(outgoing)
    turned, new_left = pl.pallas_call(
        refresh_kernel,
        out_shape=(low, wide),
        in_specs=[SMEM] + [VMEM] * 3,
        out_specs=(VMEM,) * 2,
        scratch_shapes=[
            pltpu.VMEM((side, side), jnp.float32),
            pltpu.VMEM((side, 2 * side), jnp.float32),
        ],
        name="refresh",
    )(listed, left_low, left_basis[0], incoming)
    arrived = paired(turned)
    moment_new, second_new, new_right, outward = pl.pallas_call(
        update_kernel,
        out_shape=(wide, wide, wide, low),
        in_specs=[SMEM] + [VMEM] * 7,
        out_specs=(VMEM,) * 4,
        name="update",
    )(
        listed,
        low_grad,
        first_moment[0],
        second_moment[0],
        left_basis[0],
        right_basis[0],
        new_left,
        arrived,
    )
    gathered = replica_gather(outward, replica_count)
    return (
        gathered,
        moment_new[None],
        second_new[None],
        left_new[None],
        right_new[None],
        new_left[None],
        new_right[None],
    )


def solution(mesh):
    owned = P(("shard", "replica"), None, None)
    in_specs = (P("replica", "shard", None, None),) + (owned,) * 6 + (P(),)
    out_specs = (P("shard", None, None),) + (owned,) * 6
    return jax.shard_map(local, mesh=mesh, in_specs=in_specs, out_specs=out_specs, check_vma=False)
```

```python
import jax
import jax.numpy as jnp
from jax import lax
from jax.experimental import pallas as pl
from jax.experimental.pallas import tpu as pltpu
from jax.sharding import PartitionSpec as P

POWER = 2


beta_one = 0.95
beta_two = 0.95
epsilon = 1e-08
bias_step = 10.0

TILE = 128
ROWS = 8
CHUNKS = 8
MESH = pl.DeviceIdType.MESH


def paired(block):
    count = lax.axis_size("shard")
    return lax.ppermute(block, "shard", [(low, low ^ 1) for low in range(count)])


def product(left_side, right_side, contract=(1, 0), precision=lax.Precision.HIGHEST):
    return lax.dot_general(
        left_side,
        right_side,
        (((contract[0],), (contract[1],)), ((), ())),
        precision=precision,
        preferred_element_type=jnp.float32,
    )


def low_product(left_side, right_side, contract=(1, 0)):
    return product(
        left_side.astype(jnp.bfloat16), right_side.astype(jnp.bfloat16), contract, None
    )


def inverse_factor(tile):
    side = tile.shape[0]
    spread = (ROWS, side)
    lane = lax.broadcasted_iota(jnp.int32, spread, 1)
    sub = lax.broadcasted_iota(jnp.int32, spread, 0)
    count = side // ROWS
    groups = [tile[ROWS * g : ROWS * (g + 1), :] for g in range(count)]
    finished = []
    for step in range(count):
        start = ROWS * step
        head = groups[step]
        inside = (lane >= start) & (lane < start + ROWS)
        columns = [
            jnp.broadcast_to(head[:, start + j : start + j + 1], spread) for j in range(ROWS)
        ]
        small = [
            [jnp.broadcast_to(columns[j][i : i + 1, :], spread) for j in range(i + 1)]
            for i in range(ROWS)
        ]
        lines = [
            jnp.where(
                lane == start + i,
                1.0,
                jnp.where(inside, 0.0, jnp.broadcast_to(head[i : i + 1, :], spread)),
            )
            for i in range(ROWS)
        ]
        factor = [[None] * ROWS for _ in range(ROWS)]
        inverse = []
        for j in range(ROWS):
            inverse.append(1.0 / small[j][j])
            for i in range(j + 1, ROWS):
                factor[i][j] = small[i][j] * inverse[j]
            for i in range(j + 1, ROWS):
                lines[i] = lines[i] - factor[i][j] * lines[j]
                for t in range(j + 1, i + 1):
                    small[i][t] = small[i][t] - factor[i][j] * small[t][j]
        done = jnp.zeros(spread, jnp.float32)
        for j in range(ROWS):
            done = jnp.where(sub == j, lines[j] * lax.rsqrt(small[j][j]), done)
        finished.append(jnp.where(lane < start + ROWS, done, 0.0))
        if step + 1 == count:
            break
        back = [None] * ROWS
        for j in reversed(range(ROWS)):
            value = lines[j] * inverse[j]
            for i in reversed(range(j + 1, ROWS)):
                value = value - factor[i][j] * back[i]
            back[j] = value
        for g in range(step + 1, count):
            old = groups[g]
            terms = [
                jnp.broadcast_to(old[:, start + j : start + j + 1], spread) * back[j]
                for j in range(ROWS)
            ]
            while len(terms) > 1:
                terms = [terms[t] + terms[t + 1] for t in range(0, len(terms), 2)]
            groups[g] = jnp.where(inside, 0.0, old) - terms[0]
    return jnp.concatenate(finished, 0)


def refresh_kernel(listed_ref, left_ref, left_basis_ref, incoming_ref, turned_ref, basis_ref, held, joint):
    side = left_ref.shape[0]
    listed = listed_ref[0] == 1

    @pl.when(listed)
    def _():
        held[...] = left_basis_ref[...].T

    @pl.when(jnp.logical_not(listed))
    def _():
        held[...] = incoming_ref[1].astype(jnp.float32).T

    factor = jnp.where(
        jnp.full((side, side), listed_ref[0], jnp.int32) == 1,
        left_ref[...].astype(jnp.float32),
        incoming_ref[0].astype(jnp.float32),
    ).astype(jnp.bfloat16)
    turned_ref[...] = factor

    def repeat(_, carry):
        turned = product(held[...].astype(jnp.bfloat16), turned_ref[...], precision=None)
        joint[:, side:] = turned
        for at in range(0, side, TILE):
            joint[at:, at : at + TILE] = product(turned[at:], turned[at : at + TILE], (1, 1))

        tile = joint[:TILE, :TILE]
        for block in range(side // TILE):
            at, after = block * TILE, (block + 1) * TILE
            inverse = inverse_factor(tile)
            if after < side:
                near = product(joint[after : after + TILE, at:after], inverse, (1, 1))
                tile = joint[after : after + TILE, after : after + TILE] - product(
                    near, near, (1, 1)
                )
            fresh = product(inverse, joint[at:after, side:])
            held[at:after, :] = fresh
            if after < side:
                joint[after : after + TILE, side:] -= product(near, fresh)
            if after + TILE < side:
                below = product(joint[after + TILE :, at:after], inverse, (1, 1))
                joint[after + TILE :, after : after + TILE] -= product(below, near, (1, 1))
                joint[after + TILE :, after + TILE : side] -= product(below, below, (1, 1))
                joint[after + TILE :, side:] -= product(below, fresh)
        return carry

    lax.fori_loop(0, POWER, repeat, 0)
    turned_ref[...] = held[...].T.astype(jnp.bfloat16)

    @pl.when(listed)
    def _():
        basis_ref[...] = held[...].T

    @pl.when(jnp.logical_not(listed))
    def _():
        basis_ref[...] = left_basis_ref[...]


def statistics_kernel(grad_ref, left_ref, right_ref, basis_ref, left_out, right_out, low_out, send_out):
    grad = grad_ref[...]
    rate = (1.0 - beta_two) / grad.shape[0]
    left = beta_two * left_ref[...] + rate * low_product(grad, grad, (1, 1))
    left_out[...] = left
    low_out[...] = left.astype(jnp.bfloat16)
    right = beta_two * right_ref[...] + rate * low_product(grad, grad, (0, 0))
    right_out[...] = right
    send_out[0] = right.astype(jnp.bfloat16)
    send_out[1] = basis_ref[...].astype(jnp.bfloat16)


def update_kernel(
    listed_ref,
    grad_ref,
    moment_ref,
    second_ref,
    old_left_ref,
    old_right_ref,
    left_ref,
    arrived_ref,
    moment_out,
    second_out,
    right_out,
    direction_out,
):
    listed = listed_ref[0] == 1

    @pl.when(listed)
    def _():
        right_out[...] = arrived_ref[...].astype(jnp.float32)
        plain = low_product(
            low_product(old_left_ref[...], moment_ref[...]), old_right_ref[...], (1, 1)
        )
        moment_out[...] = low_product(
            low_product(left_ref[...], plain, (0, 0)), arrived_ref[...]
        )

    @pl.when(jnp.logical_not(listed))
    def _():
        right_out[...] = old_right_ref[...]
        moment_out[...] = moment_ref[...]

    left = left_ref[...].astype(jnp.bfloat16)
    right = right_out[...].astype(jnp.bfloat16)
    rotated = low_product(low_product(left, grad_ref[...], (0, 0)), right)
    moment_new = beta_one * moment_out[...] + (1.0 - beta_one) * rotated
    second_new = beta_two * second_ref[...] + (1.0 - beta_two) * rotated * rotated
    moment_out[...] = moment_new
    second_out[...] = second_new
    scaled = (
        moment_new
        / (1.0 - beta_one**bias_step)
        / (jnp.sqrt(second_new / (1.0 - beta_two**bias_step)) + epsilon)
    )
    direction_out[...] = low_product(low_product(left, scaled), right, (1, 1)).astype(
        jnp.bfloat16
    )


def sequence(outer_count):
    return sorted(range(outer_count), key=lambda m: (m == 0, abs(2 * m - outer_count), m))


def place(outer_count):
    me = lax.axis_index("replica")
    inner = lax.rem(me, 2)
    return me, inner, me // 2, me + 1 - 2 * inner


def meet(outer_count):
    me, inner, outer, partner = place(outer_count)
    barrier = pltpu.get_barrier_semaphore()
    pl.semaphore_signal(barrier, inc=1, device_id={"replica": partner}, device_id_type=MESH)
    for m in range(1, outer_count):
        other = lax.rem(outer + m, outer_count) * 2 + inner
        pl.semaphore_signal(barrier, inc=1, device_id={"replica": other}, device_id_type=MESH)
    pl.semaphore_wait(barrier, outer_count)


def remote(source, target, send_sem, recv_sem, replica):
    return pltpu.make_async_remote_copy(
        src_ref=source,
        dst_ref=target,
        send_sem=send_sem,
        recv_sem=recv_sem,
        device_id={"replica": replica},
        device_id_type=MESH,
    )


def sum_kernel(
    grad_ref, out_ref, mine, got, pairs, far, load_sem, near_send, near_recv, far_send, far_recv
):
    outer_count = mine.shape[0]
    rows = mine.shape[1] // CHUNKS
    me, inner, outer, partner = place(outer_count)
    meet(outer_count)
    order = sequence(outer_count)
    near, loads = {}, {}
    for m in order:
        aim = lax.rem(outer + m, outer_count)
        for c in range(CHUNKS):
            part = pl.ds(c * rows, rows)
            near[m, c] = remote(
                grad_ref.at[0, aim * 2 + 1 - inner, part],
                got.at[m, part],
                near_send.at[m, c],
                near_recv.at[m, c],
                partner,
            )
            near[m, c].start()
        loads[m] = pltpu.make_async_copy(
            grad_ref.at[0, aim * 2 + inner], mine.at[m], load_sem.at[m]
        )
        loads[m].start()
    away = {}
    for m in order:
        aim = lax.rem(outer + m, outer_count)
        loads[m].wait()
        for c in range(CHUNKS):
            part = pl.ds(c * rows, rows)
            near[m, c].wait_recv()
            total = mine[m, part].astype(jnp.float32) + got[m, part].astype(jnp.float32)
            if m != 0:
                pairs[m, part] = total.astype(jnp.bfloat16)
                away[m, c] = remote(
                    pairs.at[m, part],
                    far.at[m, part],
                    far_send.at[m, c],
                    far_recv.at[m, c],
                    aim * 2 + inner,
                )
                away[m, c].start()
    for c in range(CHUNKS):
        part = pl.ds(c * rows, rows)
        total = mine[0, part].astype(jnp.float32) + got[0, part].astype(jnp.float32)
        for m in order[:-1]:
            away[m, c].wait_recv()
            total = total + far[m, part].astype(jnp.float32)
        out_ref[part] = total.astype(jnp.bfloat16)
    for copy in list(near.values()) + list(away.values()):
        copy.wait_send()


def gather_kernel(
    block_ref, out_ref, own_sem, near_send, near_recv, up_send, up_recv, down_send, down_recv
):
    outer_count = out_ref.shape[0] // 2
    rows = block_ref.shape[0] // CHUNKS
    me, inner, outer, partner = place(outer_count)
    meet(outer_count)
    keep = pltpu.make_async_copy(block_ref, out_ref.at[me], own_sem.at[0])
    keep.start()

    def above():
        return outer + 1 < outer_count

    def below():
        return outer >= 1

    def move(kind, distance, c):
        part = pl.ds(c * rows, rows)
        if kind == "up":
            sems, target, origin = (up_send, up_recv), me + 2, me - 2 * distance
        elif kind == "down":
            sems, target, origin = (down_send, down_recv), me - 2, me + 2 * distance
        else:
            sems, target, origin = (near_send, near_recv), partner, me + 2 * distance
        slot = distance + outer_count - 1 if kind == "near" else distance
        source = block_ref.at[part] if distance == 0 else out_ref.at[origin, part]
        return remote(
            source, out_ref.at[origin, part], sems[0].at[slot, c], sems[1].at[slot, c], target
        )

    for c in range(CHUNKS):
        pl.when(above())(move("up", 0, c).start)
        pl.when(below())(move("down", 0, c).start)
    for c in range(CHUNKS):
        move("near", 0, c).start()
    for distance in range(1, outer_count):
        for c in range(CHUNKS):

            @pl.when(outer >= distance)
            def _():
                move("up", distance - 1, c).wait_recv()
                pl.when(above())(move("up", distance, c).start)
                move("near", -distance, c).start()

            @pl.when(outer + distance < outer_count)
            def _():
                move("down", distance - 1, c).wait_recv()
                pl.when(below())(move("down", distance, c).start)
                move("near", distance, c).start()

    for distance in range(outer_count):
        for c in range(CHUNKS):

            @pl.when(outer >= distance)
            def _():
                move("near", -distance, c).wait()
                pl.when(above())(move("up", distance, c).wait_send)

            @pl.when(outer + distance < outer_count)
            def _():
                if distance:
                    move("near", distance, c).wait()
                pl.when(below())(move("down", distance, c).wait_send)

    keep.wait()


VMEM = pl.BlockSpec(memory_space=pltpu.VMEM)
SMEM = pl.BlockSpec(memory_space=pltpu.SMEM)
ANY = pl.BlockSpec(memory_space=pl.ANY)


def replica_sum(gradients):
    count, side = gradients.shape[1], gradients.shape[2]
    outer = count // 2
    held = pltpu.VMEM((outer, side, side), jnp.bfloat16)
    flags = pltpu.SemaphoreType.DMA((outer, CHUNKS))
    return pl.pallas_call(
        sum_kernel,
        out_shape=jax.ShapeDtypeStruct((side, side), jnp.bfloat16),
        in_specs=[ANY],
        out_specs=VMEM,
        scratch_shapes=[held] * 4 + [pltpu.SemaphoreType.DMA((outer,))] + [flags] * 4,
        compiler_params=pltpu.CompilerParams(collective_id=0, has_side_effects=True),
        name="replica_sum",
    )(gradients)


def replica_gather(block, count):
    side = block.shape[0]
    outer = count // 2
    flags = pltpu.SemaphoreType.DMA((outer, CHUNKS))
    wide = pltpu.SemaphoreType.DMA((2 * outer - 1, CHUNKS))
    return pl.pallas_call(
        gather_kernel,
        out_shape=jax.ShapeDtypeStruct((count, side, side), jnp.bfloat16),
        in_specs=[VMEM],
        out_specs=ANY,
        scratch_shapes=[pltpu.SemaphoreType.DMA((1,))] + [wide] * 2 + [flags] * 4,
        compiler_params=pltpu.CompilerParams(collective_id=1, has_side_effects=True),
        name="replica_gather",
    )(block)


def local(
    gradients,
    first_moment,
    second_moment,
    left_stat,
    right_stat,
    left_basis,
    right_basis,
    refresh_flags,
):
    replica_count = lax.axis_size("replica")
    owner_id = lax.axis_index("shard") * replica_count + lax.axis_index("replica")
    listed = lax.dynamic_slice_in_dim(refresh_flags, owner_id, 1)
    side = left_stat.shape[1]
    wide = jax.ShapeDtypeStruct((side, side), jnp.float32)
    low = jax.ShapeDtypeStruct((side, side), jnp.bfloat16)
    low_grad = replica_sum(gradients)
    left_new, right_new, left_low, outgoing = pl.pallas_call(
        statistics_kernel,
        out_shape=(wide, wide, low, jax.ShapeDtypeStruct((2, side, side), jnp.bfloat16)),
        in_specs=[VMEM] * 4,
        out_specs=(VMEM,) * 4,
        name="statistics",
    )(low_grad, left_stat[0], right_stat[0], right_basis[0])
    incoming = paired(outgoing)
    turned, new_left = pl.pallas_call(
        refresh_kernel,
        out_shape=(low, wide),
        in_specs=[SMEM] + [VMEM] * 3,
        out_specs=(VMEM,) * 2,
        scratch_shapes=[
            pltpu.VMEM((side, side), jnp.float32),
            pltpu.VMEM((side, 2 * side), jnp.float32),
        ],
        name="refresh",
    )(listed, left_low, left_basis[0], incoming)
    arrived = paired(turned)
    moment_new, second_new, new_right, outward = pl.pallas_call(
        update_kernel,
        out_shape=(wide, wide, wide, low),
        in_specs=[SMEM] + [VMEM] * 7,
        out_specs=(VMEM,) * 4,
        name="update",
    )(
        listed,
        low_grad,
        first_moment[0],
        second_moment[0],
        left_basis[0],
        right_basis[0],
        new_left,
        arrived,
    )
    gathered = replica_gather(outward, replica_count)
    return (
        gathered,
        moment_new[None],
        second_new[None],
        left_new[None],
        right_new[None],
        new_left[None],
        new_right[None],
    )


def solution(mesh):
    owned = P(("shard", "replica"), None, None)
    in_specs = (P("replica", "shard", None, None),) + (owned,) * 6 + (P(),)
    out_specs = (P("shard", None, None),) + (owned,) * 6
    return jax.shard_map(local, mesh=mesh, in_specs=in_specs, out_specs=out_specs, check_vma=False)
```
